32 devices in a mesh: group: 2 (over y), expert: 4 (over x, core), blk: 4 (over z).
Axes of the slice: x: 2, y: 2, z: 4, core: 2. Of those that a mesh axis runs over, the one named last changes fastest.
Arguments:
- tokens: bfloat16 [128, 2048], P(('group', 'expert', 'blk')), parts along dimension 0, may hold values from -6 to 6
- route_ids: int32 [128, 2], P(('group', 'expert', 'blk')), parts along dimension 0, may hold values from 0 to 3, as said below
- route_slots: int32 [128, 2], P(('group', 'expert', 'blk')), parts along dimension 0, may hold values from 0 to 3, as said below
- gate_fixed: int32 [128, 2], P(('group', 'expert', 'blk')), parts along dimension 0, may hold values from 1 to 255
- w_gate: bfloat16 [4, 2048, 8192], P('expert', None, 'blk'), may hold values from -0.125 to 0.125
- w_up: bfloat16 [4, 2048, 8192], P('expert', None, 'blk'), may hold values from -0.125 to 0.125
- w_down: bfloat16 [4, 8192, 2048], P('expert', 'blk'), may hold values from -0.125 to 0.125
Outputs:
- mixed_out: bfloat16 [128, 2048], P(('group', 'expert', 'blk')), parts along dimension 0
The draws below stay inside these ranges and needn't reach their ends.
There are 2 independent parts, one for each index of `group`. The reference program is written for one: setup_inputs(seed, part) draws one part's arguments, and reference() takes and returns one part's arrays. A program takes and returns all parts, laid end to end along the dimension named above; an argument that names none is the same for every part. Nothing has to cross between parts.
Inputs may be any that keep to these rules, and one draw needn't show every extreme that they name: `route_ids`: each row names two different experts. Among the rows of one device no expert is named more than 4 times, and one expert, the same for every device of a part, is named exactly 4 times by the rows of every device. `route_slots`: among the rows of one device, the choices that name the same expert have distinct slots.
All inputs are finite; a program needn't handle non-finite values.
Results may differ from the reference program's by a relative error of at most 0.0049.
Values may be sent and summed in bfloat16 or wider, within the bound.
No kernel may reach another device: no remote copies, remote signals or barrier semaphores. Data moves between devices by JAX's collectives and lax.ppermute only.
A program may use at most 64 MiB of HBM per device.

```python
import jax
import jax.numpy as jnp
from jax import lax

D = 2048
FF = 8192
TOK_DEV = 4
EXPERTS = 4
EXPERT_SLOTS = 4
TOKENS = 64
N_BLK = 4


def route_plan(key):
    stream = jax.random.fold_in(key, 7)
    blocks = TOKENS // TOK_DEV
    lanes_total = 2 * TOK_DEV
    busy_expert = jax.random.randint(jax.random.fold_in(stream, 1), (), 0, EXPERTS)
    expert_occupied = jnp.arange(EXPERTS, dtype=jnp.int32) == busy_expert
    weight_draw = jax.random.randint(jax.random.fold_in(stream, 2), (blocks, EXPERTS), 2, 6)
    weight_draw = jnp.where(expert_occupied[None, :], 0, weight_draw)
    remaining = lanes_total - EXPERT_SLOTS
    expert_counts = remaining * weight_draw // jnp.sum(weight_draw, axis=1, keepdims=True)
    spare_capacity = remaining - jnp.sum(expert_counts, axis=1, keepdims=True)
    partner_device = jnp.cumsum(jnp.where(expert_occupied, 0, 1)) - 1
    extra_token_flag = jnp.where(expert_occupied[None, :], 0, (partner_device[None, :] < spare_capacity).astype(jnp.int32))
    expert_counts = jnp.where(expert_occupied[None, :], EXPERT_SLOTS, expert_counts + extra_token_flag).astype(jnp.int32)
    run_ends = jnp.cumsum(expert_counts, axis=1)
    starts = run_ends - expert_counts
    position = jnp.arange(lanes_total, dtype=jnp.int32)
    labels = jnp.sum((position[None, :, None] >= run_ends[:, None, :]).astype(jnp.int32), axis=2)
    within = position[None, :] - jnp.take_along_axis(starts, labels, axis=1)
    slot_score = jax.random.randint(jax.random.fold_in(stream, 3), (blocks, EXPERTS, EXPERT_SLOTS), 0, 4096) * EXPERT_SLOTS + jnp.arange(EXPERT_SLOTS, dtype=jnp.int32)
    slot_perm = jnp.argsort(slot_score, axis=2, stable=True).astype(jnp.int32).reshape(blocks, EXPERTS * EXPERT_SLOTS)
    slot_of = jnp.take_along_axis(slot_perm, labels * EXPERT_SLOTS + within, axis=1)
    token_priority = jax.random.randint(jax.random.fold_in(stream, 4), (blocks, TOK_DEV), 0, 4096) * TOK_DEV + jnp.arange(TOK_DEV, dtype=jnp.int32)
    token_perm = jnp.argsort(token_priority, axis=1, stable=True).astype(jnp.int32)
    expert_pair = jnp.stack([labels[:, :TOK_DEV], labels[:, TOK_DEV:]], axis=2)
    slot_pair = jnp.stack([slot_of[:, :TOK_DEV], slot_of[:, TOK_DEV:]], axis=2)
    expert_pair = jnp.take_along_axis(expert_pair, token_perm[:, :, None], axis=1)
    slot_pair = jnp.take_along_axis(slot_pair, token_perm[:, :, None], axis=1)
    return (expert_pair.reshape(TOKENS, 2).astype(jnp.int32), slot_pair.reshape(TOKENS, 2).astype(jnp.int32))


def draw_route_ids(key, part):
    return route_plan(key)[0]


def draw_route_slots(key, part):
    return route_plan(key)[1]


def touch_ends(array, own_key, smallest, largest):
    shape = array.shape
    spot = [jax.random.randint(jax.random.fold_in(own_key, axis), (), 0, shape[axis]) for axis in range(len(shape))]
    array = array.at[tuple(spot)].set(smallest)
    longest = shape.index(max(shape))
    spot[longest] = (spot[longest] + 1) % shape[longest]
    return array.at[tuple(spot)].set(largest)


def steps_of(stream_key, dims, split, least, high):
    def one(dim, shards_of):
        draws = jax.random.uniform(jax.random.fold_in(jax.random.fold_in(stream_key, 6), dim), (shards_of,), jnp.float32, least / len(split), high / len(split))
        return jnp.repeat(jnp.exp(draws), dims[dim] // shards_of).reshape((-1,) + (1,) * (len(dims) - dim - 1))

    loudness = one(*split[0])
    for cut in split[1:]:
        loudness = loudness * one(*cut)
    return loudness


def centred(own_key, dims, scale, limit, cuts=(), held_as=jnp.bfloat16):
    values = scale * jax.random.normal(own_key, dims, jnp.float32)
    if cuts:
        values = values * steps_of(own_key, dims, cuts, -0.22, 0.18)
    return jnp.clip(values, -limit, limit).astype(held_as)


def setup_inputs(seed: int = 0, part: int = 0) -> dict:
    seeds = jax.random.split(jax.random.key(seed), 8)
    part_keys = jax.random.split(jax.random.fold_in(seeds[7], part), 8)
    return {
        "tokens": centred(part_keys[0], (TOKENS, D), 1.0, 6.0, ((0, 16),)),
        "route_ids": draw_route_ids(jax.random.fold_in(jax.random.fold_in(seeds[7], part), 71), part),
        "route_slots": draw_route_slots(jax.random.fold_in(jax.random.fold_in(seeds[7], part), 71), part),
        "gate_fixed": touch_ends(jax.random.randint(part_keys[3], (TOKENS, 2), 1, 256), jax.random.fold_in(part_keys[3], 1), 1, 255).astype(jnp.int32),
        "w_gate": centred(seeds[4], (EXPERTS, D, FF), D ** -0.5, 0.125, ((0, 4), (2, 4))),
        "w_up": centred(seeds[5], (EXPERTS, D, FF), D ** -0.5, 0.125, ((0, 4), (2, 4))),
        "w_down": centred(seeds[6], (EXPERTS, FF, D), (FF // 4) ** -0.5, 0.125, ((0, 4), (1, 4))),
    }


def expert_ffn(row_data, gate_mat, up_mat, down_mat):
    width = row_data.shape[1]
    slice_width = FF // N_BLK
    gate_slices = gate_mat.reshape(width, N_BLK, slice_width).transpose(1, 0, 2)
    up_slices = up_mat.reshape(width, N_BLK, slice_width).transpose(1, 0, 2)
    down_slices = down_mat.reshape(N_BLK, slice_width, width)

    def add_slice(total, mats):
        gate_part = jnp.dot(row_data, mats[0], preferred_element_type=jnp.float32)
        up_part = jnp.dot(row_data, mats[1], preferred_element_type=jnp.float32)
        hidden = (jax.nn.silu(gate_part) * up_part).astype(jnp.bfloat16)
        partial_value = jnp.dot(hidden, mats[2], preferred_element_type=jnp.float32)
        return total + partial_value, None

    start_total = jnp.zeros((row_data.shape[0], width), jnp.float32)
    total, unused = lax.scan(add_slice, start_total, (gate_slices, up_slices, down_slices))
    return total


def reference(tokens, route_ids, route_slots, gate_fixed, w_gate, w_up, w_down):
    blocks = TOKENS // TOK_DEV
    owners = (jnp.arange(TOKENS, dtype=jnp.int32) // TOK_DEV).astype(jnp.int32)[:, None]
    slot_place = (route_ids * (blocks * EXPERT_SLOTS) + owners * EXPERT_SLOTS + route_slots).astype(jnp.int32)
    buffer = jnp.zeros((EXPERTS * blocks * EXPERT_SLOTS, D), jnp.bfloat16)
    buffer = buffer.at[slot_place.reshape(-1)].set(jnp.repeat(tokens, 2, axis=0))
    stacked = buffer.reshape(EXPERTS, blocks * EXPERT_SLOTS, D)
    expert_out = lax.map(lambda items: expert_ffn(items[0], items[1], items[2], items[3]), (stacked, w_gate, w_up, w_down))
    flat_out = expert_out.reshape(EXPERTS * blocks * EXPERT_SLOTS, D)
    picked = flat_out[slot_place]
    shares = gate_fixed.astype(jnp.float32)
    shares = shares / jnp.sum(shares, axis=1, keepdims=True)
    mixed_out = jnp.sum(shares[:, :, None] * picked, axis=1)
    return mixed_out.astype(jnp.bfloat16)
```

```python
import functools

import jax
import jax.numpy as jnp
from jax import lax
from jax.experimental import pallas as pl
from jax.experimental.pallas import tpu as pltpu
from jax.sharding import PartitionSpec as P

VMEM = pl.BlockSpec(memory_space=pltpu.VMEM)
ANY = pl.BlockSpec(memory_space=pl.ANY)


def peer(i, d, n):
    return i ^ d if n & (n - 1) == 0 else (i + d) % n


def source(i, d, n):
    return i ^ d if n & (n - 1) == 0 else (i - d) % n


def fetch(x, axis, d):
    n = lax.axis_size(axis)
    return lax.ppermute(x, axis, [(peer(i, d, n), i) for i in range(n)])


def deliver(x, axis, d):
    n = lax.axis_size(axis)
    return lax.ppermute(x, axis, [(i, peer(i, d, n)) for i in range(n)])


def stack_kernel(*refs):
    out = refs[-1]
    rows = [r[...].astype(jnp.float32) for r in refs[:-1]]
    out[...] = jnp.concatenate(rows, axis=0).astype(out.dtype)


def stack(blocks):
    rows = sum(b.shape[0] for b in blocks)
    return pl.pallas_call(
        stack_kernel,
        name="stack",
        out_shape=jax.ShapeDtypeStruct((rows, blocks[0].shape[1]), blocks[0].dtype),
        in_specs=[VMEM] * len(blocks),
        out_specs=VMEM,
    )(*blocks)


def ffn_kernel(n_e, n_b, count, chunks, *refs):
    xs = refs[:n_e]
    gate_hbm, up_hbm, down_hbm = refs[n_e : n_e + 3]
    outs = refs[n_e + 3 : n_e + 3 + n_b]
    gate_w, up_w, down_w, gate_acc, up_acc, sems = refs[n_e + 3 + n_b :]
    depth, inner = gate_w.shape[0] // chunks, down_w.shape[0] // chunks
    copies = {}
    for c in range(chunks):
        for which, (src, dst) in enumerate(((gate_hbm, gate_w), (up_hbm, up_w))):
            rows = pl.ds(c * depth, depth)
            copies[which, c] = pltpu.make_async_copy(src.at[0, rows, :], dst.at[rows, :], sems.at[which, c])
            copies[which, c].start()
    for c in range(chunks):
        rows = pl.ds(c * inner, inner)
        copies[2, c] = pltpu.make_async_copy(down_hbm.at[0, rows, :], down_w.at[rows, :], sems.at[2, c])
        copies[2, c].start()
    x = jnp.concatenate([r[...] for r in xs], axis=0)
    for c in range(chunks):
        cut = slice(c * depth, (c + 1) * depth)
        for which, (w, acc) in enumerate(((gate_w, gate_acc), (up_w, up_acc))):
            copies[which, c].wait()
            part = jnp.dot(x[:, cut], w[cut, :], preferred_element_type=jnp.float32)
            acc[...] = part if c == 0 else acc[...] + part
    v = gate_acc[...]
    hidden = (v / (1.0 + jnp.exp(-v)) * up_acc[...]).astype(jnp.bfloat16)
    total = None
    for c in range(chunks):
        cut = slice(c * inner, (c + 1) * inner)
        copies[2, c].wait()
        part = jnp.dot(hidden[:, cut], down_w[cut, :], preferred_element_type=jnp.float32)
        total = part if c == 0 else total + part
    for d, out in enumerate(outs):
        rows = [total[(m * n_b + d) * count : (m * n_b + d + 1) * count] for m in range(n_e)]
        out[...] = jnp.concatenate(rows, axis=0).astype(out.dtype)


def ffn(xs, w_gate, w_up, w_down, n_b, count):
    n_e, (rows, width) = len(xs), xs[0].shape
    hidden = w_gate.shape[2]
    chunks = 4 if hidden % 512 == 0 else 1
    out_shape = [
        jax.ShapeDtypeStruct((n_e * count, width), jnp.float32 if d == 0 else jnp.bfloat16) for d in range(n_b)
    ]
    return pl.pallas_call(
        functools.partial(ffn_kernel, n_e, n_b, count, chunks),
        name="ffn",
        out_shape=out_shape,
        in_specs=[VMEM] * n_e + [ANY] * 3,
        out_specs=[VMEM] * n_b,
        scratch_shapes=[
            pltpu.VMEM(w_gate.shape[1:], w_gate.dtype),
            pltpu.VMEM(w_up.shape[1:], w_up.dtype),
            pltpu.VMEM(w_down.shape[1:], w_down.dtype),
            pltpu.VMEM((n_e * rows, hidden), jnp.float32),
            pltpu.VMEM((n_e * rows, hidden), jnp.float32),
            pltpu.SemaphoreType.DMA((3, chunks)),
        ],
    )(*xs, w_gate, w_up, w_down)


def merge_kernel(n_b, *refs):
    total = refs[0][...]
    for r in refs[1:n_b]:
        total = total + r[...].astype(jnp.float32)
    outs = refs[n_b:]
    count = total.shape[0] // len(outs)
    for m, out in enumerate(outs):
        out[...] = total[m * count : (m + 1) * count].astype(out.dtype)


def merge(parts, n_e):
    rows, width = parts[0].shape
    return pl.pallas_call(
        functools.partial(merge_kernel, len(parts)),
        name="merge",
        out_shape=[jax.ShapeDtypeStruct((rows // n_e, width), jnp.bfloat16)] * n_e,
        in_specs=[VMEM] * len(parts),
        out_specs=[VMEM] * n_e,
    )(*parts)


def on_device(tokens, route_ids, route_slots, gate_fixed, w_gate, w_up, w_down):
    count = tokens.shape[0]
    n_e, n_b = lax.axis_size("expert"), lax.axis_size("blk")
    fixed = gate_fixed.astype(jnp.float32)
    shares = fixed / jnp.sum(fixed, axis=1, keepdims=True)
    me = lax.axis_index("expert")
    mine = stack([tokens] + [fetch(tokens, "blk", d) for d in range(1, n_b)])
    xs = [mine] + [fetch(mine, "expert", m) for m in range(1, n_e)]
    parts = ffn(xs, w_gate, w_up, w_down, n_b, count)
    parts = [parts[0]] + [deliver(parts[d], "blk", d) for d in range(1, n_b)]
    blocks = merge(parts, n_e)
    blocks = [blocks[0]] + [deliver(blocks[m], "expert", m) for m in range(1, n_e)]
    mixed = 0.0
    for m, block in enumerate(blocks):
        share = jnp.sum(jnp.where(route_ids == source(me, m, n_e), shares, 0.0), axis=1, keepdims=True)
        mixed = mixed + share * block.astype(jnp.float32)
    return mixed.astype(jnp.bfloat16)


def solution(mesh):
    return jax.shard_map(
        on_device,
        mesh=mesh,
        in_specs=(
            P(("group", "expert", "blk"), None),
            P(("group", "expert", "blk"), None),
            P(("group", "expert", "blk"), None),
            P(("group", "expert", "blk"), None),
            P("expert", None, "blk"),
            P("expert", None, "blk"),
            P("expert", "blk", None),
        ),
        out_specs=P(("group", "expert", "blk"), None),
        check_vma=False,
    )
```

```python
import functools

import jax
import jax.numpy as jnp
from jax import lax
from jax.experimental import pallas as pl
from jax.experimental.pallas import tpu as pltpu
from jax.sharding import PartitionSpec as P

VMEM = pl.BlockSpec(memory_space=pltpu.VMEM)
ANY = pl.BlockSpec(memory_space=pl.ANY)


def peer(i, d, n):
    return i ^ d if n & (n - 1) == 0 else (i + d) % n


def source(i, d, n):
    return i ^ d if n & (n - 1) == 0 else (i - d) % n


def fetch(x, axis, d):
    n = lax.axis_size(axis)
    return lax.ppermute(x, axis, [(peer(i, d, n), i) for i in range(n)])


def deliver(x, axis, d):
    n = lax.axis_size(axis)
    return lax.ppermute(x, axis, [(i, peer(i, d, n)) for i in range(n)])


def stack_kernel(*refs):
    out = refs[-1]
    rows = [r[...].astype(jnp.float32) for r in refs[:-1]]
    out[...] = jnp.concatenate(rows, axis=0).astype(out.dtype)


def stack(blocks):
    rows = sum(b.shape[0] for b in blocks)
    return pl.pallas_call(
        stack_kernel,
        name="stack",
        compiler_params=pltpu.CompilerParams(vmem_limit_bytes=8 << 20),
        out_shape=jax.ShapeDtypeStruct((rows, blocks[0].shape[1]), blocks[0].dtype),
        in_specs=[VMEM] * len(blocks),
        out_specs=VMEM,
    )(*blocks)


def prefetch_kernel(chunks, with_rows, *refs):
    sems, dst = refs[-1], refs[-2 - with_rows]
    depth = dst.shape[0] // chunks
    copies = []
    if with_rows:
        copies.append(pltpu.make_async_copy(refs[1], refs[-2], sems.at[chunks]))
    for c in range(chunks):
        rows = pl.ds(c * depth, depth)
        copies.append(pltpu.make_async_copy(refs[0].at[0, rows, :], dst.at[rows, :], sems.at[c]))
    for copy in copies:
        copy.start()
    for copy in copies:
        copy.wait()


def in_hbm(w):
    return pltpu.with_memory_space_constraint(w, pltpu.HBM)


def in_vmem(w):
    return pltpu.with_memory_space_constraint(w, pltpu.VMEM)


def prefetch(w, rows=None, after=None):
    chunks = 4 if w.shape[1] % 512 == 0 else 1
    more = [x for x in (rows, after) if x is not None]
    out_shape = [pltpu.VMEM(w.shape[1:], w.dtype)]
    if rows is not None:
        out_shape.append(pltpu.VMEM(rows.shape, rows.dtype))
        more = [in_hbm(rows)]
    return pl.pallas_call(
        functools.partial(prefetch_kernel, chunks, rows is not None),
        name="prefetch",
        compiler_params=pltpu.CompilerParams(vmem_limit_bytes=1 << 20),
        cost_estimate=pl.CostEstimate(flops=0, transcendentals=0, bytes_accessed=w.size * 4),
        out_shape=out_shape,
        in_specs=[ANY] * (1 + len(more)),
        out_specs=[VMEM] * len(out_shape),
        scratch_shapes=[pltpu.SemaphoreType.DMA((chunks + 1,))],
    )(in_hbm(w), *more)


def ffn_kernel(n_e, n_b, count, chunks, *refs):
    xs = refs[:n_e]
    gate_w, up_w, down_hbm = refs[n_e : n_e + 3]
    outs = refs[n_e + 3 : n_e + 3 + n_b]
    down_w, sems = refs[n_e + 3 + n_b :]
    inner = down_w.shape[0] // chunks
    copies = []
    for c in range(chunks):
        rows = pl.ds(c * inner, inner)
        copies.append(pltpu.make_async_copy(down_hbm.at[0, rows, :], down_w.at[rows, :], sems.at[c]))
        copies[c].start()
    x = jnp.concatenate([r[...] for r in xs], axis=0)
    total = None
    for c in range(chunks):
        cut = slice(c * inner, (c + 1) * inner)
        v = jnp.dot(x, gate_w[:, cut], preferred_element_type=jnp.float32)
        u = jnp.dot(x, up_w[:, cut], preferred_element_type=jnp.float32)
        hidden = (v / (1.0 + jnp.exp(-v)) * u).astype(jnp.bfloat16)
        copies[c].wait()
        part = jnp.dot(hidden, down_w[cut, :], preferred_element_type=jnp.float32)
        total = part if c == 0 else total + part
    for d, out in enumerate(outs):
        rows = [total[(m * n_b + d) * count : (m * n_b + d + 1) * count] for m in range(n_e)]
        out[...] = jnp.concatenate(rows, axis=0).astype(out.dtype)


def ffn(xs, w_gate, w_up, w_down, n_b, count):
    n_e, width = len(xs), xs[0].shape[1]
    hidden = w_gate.shape[1]
    chunks = 4 if hidden % 512 == 0 else 1
    out_shape = [
        jax.ShapeDtypeStruct((n_e * count, width), jnp.float32 if d == 0 else jnp.bfloat16) for d in range(n_b)
    ]
    return pl.pallas_call(
        functools.partial(ffn_kernel, n_e, n_b, count, chunks),
        name="ffn",
        compiler_params=pltpu.CompilerParams(vmem_limit_bytes=16 << 20),
        out_shape=out_shape,
        in_specs=[VMEM] * (n_e + 2) + [ANY],
        out_specs=[VMEM] * n_b,
        scratch_shapes=[
            pltpu.VMEM(w_down.shape[1:], w_down.dtype),
            pltpu.SemaphoreType.DMA((chunks,)),
        ],
    )(*xs, in_vmem(w_gate), in_vmem(w_up), in_hbm(w_down))


def merge_kernel(n_b, *refs):
    total = refs[0][...]
    for r in refs[1:n_b]:
        total = total + r[...].astype(jnp.float32)
    outs = refs[n_b:]
    count = total.shape[0] // len(outs)
    for m, out in enumerate(outs):
        out[...] = total[m * count : (m + 1) * count].astype(out.dtype)


def merge(parts, n_e):
    rows, width = parts[0].shape
    return pl.pallas_call(
        functools.partial(merge_kernel, len(parts)),
        name="merge",
        compiler_params=pltpu.CompilerParams(vmem_limit_bytes=8 << 20),
        out_shape=[jax.ShapeDtypeStruct((rows // n_e, width), jnp.bfloat16)] * n_e,
        in_specs=[VMEM] * len(parts),
        out_specs=[VMEM] * n_e,
    )(*parts)


def mix_kernel(n_e, ids_ref, fixed_ref, *refs):
    blocks, out = refs[:-1], refs[-1]
    me = lax.axis_index("expert")
    ids = ids_ref[...]
    fixed = fixed_ref[...].astype(jnp.float32)
    shares = fixed / jnp.sum(fixed, axis=1, keepdims=True)
    mixed = None
    for m, block in enumerate(blocks):
        share = jnp.sum(jnp.where(ids == source(me, m, n_e), shares, 0.0), axis=1, keepdims=True)
        part = share * block[...].astype(jnp.float32)
        mixed = part if m == 0 else mixed + part
    out[...] = mixed.astype(out.dtype)


def mix(route_ids, gate_fixed, blocks):
    return pl.pallas_call(
        functools.partial(mix_kernel, len(blocks)),
        name="mix",
        compiler_params=pltpu.CompilerParams(vmem_limit_bytes=4 << 20),
        out_shape=jax.ShapeDtypeStruct(blocks[0].shape, jnp.bfloat16),
        in_specs=[VMEM] * (2 + len(blocks)),
        out_specs=VMEM,
    )(route_ids, gate_fixed, *blocks)


def on_device(tokens, route_ids, route_slots, gate_fixed, w_gate, w_up, w_down):
    count = tokens.shape[0]
    n_e, n_b = lax.axis_size("expert"), lax.axis_size("blk")
    others = [fetch(tokens, "blk", d) for d in range(1, n_b)]
    gate_w, own = prefetch(w_gate, rows=tokens)
    mine = stack([own] + others)
    (up_w,) = prefetch(w_up, after=mine)
    xs = [mine] + [fetch(mine, "expert", m) for m in range(1, n_e)]
    parts = ffn(xs, gate_w, up_w, w_down, n_b, count)
    parts = [parts[0]] + [deliver(parts[d], "blk", d) for d in range(1, n_b)]
    blocks = merge(parts, n_e)
    blocks = [blocks[0]] + [deliver(blocks[m], "expert", m) for m in range(1, n_e)]
    return mix(route_ids, gate_fixed, blocks)


def solution(mesh):
    return jax.shard_map(
        on_device,
        mesh=mesh,
        in_specs=(
            P(("group", "expert", "blk"), None),
            P(("group", "expert", "blk"), None),
            P(("group", "expert", "blk"), None),
            P(("group", "expert", "blk"), None),
            P("expert", None, "blk"),
            P("expert", None, "blk"),
            P("expert", "blk", None),
        ),
        out_specs=P(("group", "expert", "blk"), None),
        check_vma=False,
    )
```

```python
import functools
import math

import jax
import jax.numpy as jnp
from jax import lax
from jax.experimental import pallas as pl
from jax.experimental.pallas import tpu as pltpu
from jax.sharding import PartitionSpec as P

ROWS = 128
VMEM = pl.BlockSpec(memory_space=pltpu.VMEM)
ANY = pl.BlockSpec(memory_space=pl.ANY)


def peer(i, d, n):
    return i ^ d if n & (n - 1) == 0 else (i + d) % n


def source(i, d, n):
    return i ^ d if n & (n - 1) == 0 else (i - d) % n


def fetch(x, axis, d):
    n = lax.axis_size(axis)
    return lax.ppermute(x, axis, [(peer(i, d, n), i) for i in range(n)])


def deliver(x, axis, d):
    n = lax.axis_size(axis)
    return lax.ppermute(x, axis, [(i, peer(i, d, n)) for i in range(n)])


def stack_kernel(*refs):
    out = refs[-1]
    rows = [r[...].astype(jnp.float32) for r in refs[:-1]]
    out[...] = jnp.concatenate(rows, axis=0).astype(out.dtype)


def stack(blocks):
    rows = sum(b.shape[0] for b in blocks)
    return pl.pallas_call(
        stack_kernel,
        name="stack",
        compiler_params=pltpu.CompilerParams(vmem_limit_bytes=8 << 20),
        out_shape=jax.ShapeDtypeStruct((rows, blocks[0].shape[1]), blocks[0].dtype),
        in_specs=[VMEM] * len(blocks),
        out_specs=VMEM,
    )(*blocks)


def prefetch_kernel(cuts, *refs):
    sems, dsts = refs[-1], refs[-1 - len(cuts) : -1]
    copies = []
    for i, (cut, dst) in enumerate(zip(cuts, dsts, strict=True)):
        src = refs[i] if cut is None else refs[i].at[0, pl.ds(cut, dst.shape[0]), :]
        copies.append(pltpu.make_async_copy(src, dst, sems.at[i]))
        copies[i].start()
    for copy in copies:
        copy.wait()


def in_hbm(w):
    return pltpu.with_memory_space_constraint(w, pltpu.HBM)


def in_vmem(w):
    return pltpu.with_memory_space_constraint(w, pltpu.VMEM)


def halves(w):
    rows = w.shape[1] // 2
    return (w, 0, rows), (w, rows, rows)


def prefetch(*pieces, after=None):
    arrays, cuts, out_shape = [], [], []
    for w, first, rows in pieces:
        arrays.append(in_hbm(w))
        cuts.append(first)
        out_shape.append(pltpu.VMEM(w.shape if first is None else (rows, w.shape[2]), w.dtype))
    if after is not None:
        arrays.append(after)
    moved = sum(2 * math.prod(o.shape) * o.dtype.itemsize for o in out_shape)
    return pl.pallas_call(
        functools.partial(prefetch_kernel, tuple(cuts)),
        name="prefetch",
        compiler_params=pltpu.CompilerParams(vmem_limit_bytes=1 << 20),
        cost_estimate=pl.CostEstimate(flops=0, transcendentals=0, bytes_accessed=moved),
        out_shape=out_shape,
        in_specs=[ANY] * len(arrays),
        out_specs=[VMEM] * len(pieces),
        scratch_shapes=[pltpu.SemaphoreType.DMA((len(pieces),))],
    )(*arrays)


def product(x, pieces):
    total, first = None, 0
    for w in pieces:
        part = jnp.dot(x[:, first : first + w.shape[0]], w[...], preferred_element_type=jnp.float32)
        total = part if total is None else total + part
        first += w.shape[0]
    return total


def ffn_kernel(n_e, n_b, count, held, cuts, *refs):
    xs, refs = refs[:n_e], refs[n_e:]
    loaded, refs = refs[: sum(held)], refs[sum(held) :]
    sources, refs = refs[: len(cuts)], refs[len(cuts) :]
    outs, refs = refs[:n_b], refs[n_b:]
    rest, sems = refs[:-1], refs[-1]
    copies = []
    for i, (cut, src, dst) in enumerate(zip(cuts, sources, rest, strict=True)):
        copies.append(pltpu.make_async_copy(src.at[0, pl.ds(cut, dst.shape[0]), :], dst, sems.at[i]))
        copies[i].start()
    gate_w, up_w, down_w = loaded[: held[0]], loaded[held[0] : held[0] + held[1]], loaded[held[0] + held[1] :]
    x = jnp.concatenate([r[...] for r in xs], axis=0)
    rows = x.shape[0]
    spare = -rows % ROWS
    if spare:
        x = jnp.concatenate([x, jnp.zeros((spare, x.shape[1]), x.dtype)], axis=0)
    v, u = product(x, gate_w), product(x, up_w)
    hidden = (v / (1.0 + jnp.exp(-v)) * u).astype(jnp.bfloat16)
    total = product(hidden, down_w) if down_w else 0.0
    first = sum(w.shape[0] for w in down_w)
    for copy, w in zip(copies, rest, strict=True):
        copy.wait()
        total = total + product(hidden[:, first : first + w.shape[0]], [w])
        first += w.shape[0]
    for d, out in enumerate(outs):
        part = [total[(m * n_b + d) * count : (m * n_b + d + 1) * count] for m in range(n_e)]
        out[...] = jnp.concatenate(part, axis=0).astype(out.dtype)


def ffn(xs, gate_w, up_w, down_w, rest, n_b, count):
    n_e, width = len(xs), xs[0].shape[1]
    out_shape = [
        jax.ShapeDtypeStruct((n_e * count, width), jnp.float32 if d == 0 else jnp.bfloat16) for d in range(n_b)
    ]
    loaded = [in_vmem(w) for w in (*gate_w, *up_w, *down_w)]
    held = (len(gate_w), len(up_w), len(down_w))
    return pl.pallas_call(
        functools.partial(ffn_kernel, n_e, n_b, count, held, tuple(first for _, first, _ in rest)),
        name="ffn",
        compiler_params=pltpu.CompilerParams(vmem_limit_bytes=20 << 20),
        out_shape=out_shape,
        in_specs=[VMEM] * (n_e + len(loaded)) + [ANY] * len(rest),
        out_specs=[VMEM] * n_b,
        scratch_shapes=[pltpu.VMEM((rows, w.shape[2]), w.dtype) for w, _, rows in rest]
        + [pltpu.SemaphoreType.DMA((max(len(rest), 1),))],
    )(*xs, *loaded, *[in_hbm(w) for w, _, _ in rest])


def merge_kernel(n_b, *refs):
    total = refs[0][...]
    for r in refs[1:n_b]:
        total = total + r[...].astype(jnp.float32)
    outs = refs[n_b:]
    count = total.shape[0] // len(outs)
    for m, out in enumerate(outs):
        out[...] = total[m * count : (m + 1) * count].astype(out.dtype)


def merge(parts, n_e):
    rows, width = parts[0].shape
    return pl.pallas_call(
        functools.partial(merge_kernel, len(parts)),
        name="merge",
        compiler_params=pltpu.CompilerParams(vmem_limit_bytes=8 << 20),
        out_shape=[jax.ShapeDtypeStruct((rows // n_e, width), jnp.bfloat16)] * n_e,
        in_specs=[VMEM] * len(parts),
        out_specs=[VMEM] * n_e,
    )(*parts)


def mix_kernel(n_e, ids_ref, fixed_ref, *refs):
    blocks, out = refs[:-1], refs[-1]
    me = lax.axis_index("expert")
    ids = ids_ref[...]
    fixed = fixed_ref[...].astype(jnp.float32)
    shares = fixed / jnp.sum(fixed, axis=1, keepdims=True)
    mixed = None
    for m, block in enumerate(blocks):
        share = jnp.sum(jnp.where(ids == source(me, m, n_e), shares, 0.0), axis=1, keepdims=True)
        part = share * block[...].astype(jnp.float32)
        mixed = part if m == 0 else mixed + part
    out[...] = mixed.astype(out.dtype)


def mix(route_ids, gate_fixed, blocks):
    return pl.pallas_call(
        functools.partial(mix_kernel, len(blocks)),
        name="mix",
        compiler_params=pltpu.CompilerParams(vmem_limit_bytes=4 << 20),
        out_shape=jax.ShapeDtypeStruct(blocks[0].shape, jnp.bfloat16),
        in_specs=[VMEM] * (2 + len(blocks)),
        out_specs=VMEM,
    )(route_ids, gate_fixed, *blocks)


def on_device(tokens, route_ids, route_slots, gate_fixed, w_gate, w_up, w_down):
    count = tokens.shape[0]
    n_e, n_b = lax.axis_size("expert"), lax.axis_size("blk")
    others = [fetch(tokens, "blk", d) for d in range(1, n_b)]
    gate_a, gate_b, up_a, own = prefetch(*halves(w_gate), halves(w_up)[0], (tokens, None, 0))
    mine = stack([own] + others)
    up_b, down_a = prefetch(halves(w_up)[1], halves(w_down)[0], after=mine)
    xs = [mine] + [fetch(mine, "expert", m) for m in range(1, n_e)]
    parts = ffn(xs, [gate_a, gate_b], [up_a, up_b], [down_a], halves(w_down)[1:], n_b, count)
    parts = [parts[0]] + [deliver(parts[d], "blk", d) for d in range(1, n_b)]
    blocks = merge(parts, n_e)
    blocks = [blocks[0]] + [deliver(blocks[m], "expert", m) for m in range(1, n_e)]
    return mix(route_ids, gate_fixed, blocks)


def solution(mesh):
    return jax.shard_map(
        on_device,
        mesh=mesh,
        in_specs=(
            P(("group", "expert", "blk"), None),
            P(("group", "expert", "blk"), None),
            P(("group", "expert", "blk"), None),
            P(("group", "expert", "blk"), None),
            P("expert", None, "blk"),
            P("expert", None, "blk"),
            P("expert", "blk", None),
        ),
        out_specs=P(("group", "expert", "blk"), None),
        check_vma=False,
    )
```

```python
import functools

import jax
import jax.numpy as jnp
from jax import lax
from jax.experimental import pallas as pl
from jax.experimental.pallas import tpu as pltpu
from jax.sharding import PartitionSpec as P

ROWS = 128
HINT = 2 * 10**10
VMEM = pl.BlockSpec(memory_space=pltpu.VMEM)
ANY = pl.BlockSpec(memory_space=pl.ANY)


def limit(mib):
    return pltpu.CompilerParams(vmem_limit_bytes=mib << 20)


def peer(i, d, n):
    return i ^ d if n & (n - 1) == 0 else (i + d) % n


def source(i, d, n):
    return i ^ d if n & (n - 1) == 0 else (i - d) % n


def fetch(x, axis, d):
    n = lax.axis_size(axis)
    return lax.ppermute(x, axis, [(peer(i, d, n), i) for i in range(n)])


def deliver(x, axis, d):
    n = lax.axis_size(axis)
    return lax.ppermute(x, axis, [(i, peer(i, d, n)) for i in range(n)])


def last_first(n):
    return [0, n - 1, *range(1, n - 1)]


def first_last(n):
    return [0, *range(2, n), 1]


def half_first(n):
    return [0, n // 2, *(i for i in range(1, n) if i != n // 2)]


def restored(refs, order):
    got = [None] * len(order)
    for ref, i in zip(refs, order, strict=True):
        got[i] = ref
    return got


def rows_kernel(src, dst, sem):
    copy = pltpu.make_async_copy(src, dst, sem)
    copy.start()
    copy.wait()


def on_chip(x):
    return pl.pallas_call(
        rows_kernel,
        name="rows",
        compiler_params=limit(1),
        cost_estimate=pl.CostEstimate(flops=0, transcendentals=0, bytes_accessed=4 * x.size),
        out_shape=pltpu.VMEM(x.shape, x.dtype),
        in_specs=[ANY],
        out_specs=VMEM,
        scratch_shapes=[pltpu.SemaphoreType.DMA],
    )(pltpu.with_memory_space_constraint(x, pltpu.HBM))


def stack_kernel(upper, lower, out):
    rows = [r[...].astype(jnp.float32) for r in (upper, lower)]
    out[...] = jnp.concatenate(rows, axis=0).astype(out.dtype)


def stack(upper, lower):
    rows = upper.shape[0] + lower.shape[0]
    return pl.pallas_call(
        stack_kernel,
        name="stack",
        compiler_params=limit(1 if rows * upper.shape[1] < 2**16 else 8),
        cost_estimate=pl.CostEstimate(flops=HINT, transcendentals=0, bytes_accessed=0),
        out_shape=jax.ShapeDtypeStruct((rows, upper.shape[1]), upper.dtype),
        in_specs=[VMEM] * 2,
        out_specs=VMEM,
    )(upper, lower)


def ffn_kernel(order, n_b, count, *refs):
    n_e = len(order)
    xs, (gate_w, up_w, down_w), outs = restored(refs[:n_e], order), refs[n_e : n_e + 3], refs[n_e + 3 :]
    x = jnp.concatenate([r[...] for r in xs], axis=0)
    spare = -x.shape[0] % ROWS
    if spare:
        x = jnp.concatenate([x, jnp.zeros((spare, x.shape[1]), x.dtype)], axis=0)
    v = jnp.dot(x, gate_w[0], preferred_element_type=jnp.float32)
    u = jnp.dot(x, up_w[0], preferred_element_type=jnp.float32)
    hidden = (v / (1.0 + jnp.exp(-v)) * u).astype(jnp.bfloat16)
    total = jnp.dot(hidden, down_w[0], preferred_element_type=jnp.float32)
    for d, out in enumerate(outs):
        part = [total[(m * n_b + d) * count : (m * n_b + d + 1) * count] for m in range(n_e)]
        out[...] = jnp.concatenate(part, axis=0).astype(out.dtype)


def ffn(xs, w_gate, w_up, w_down, n_b, count):
    n_e, (rows, width) = len(xs), xs[0].shape
    order = last_first(n_e)
    out_shape = [
        jax.ShapeDtypeStruct((n_e * count, width), jnp.float32 if d == 0 else jnp.bfloat16) for d in range(n_b)
    ]
    return pl.pallas_call(
        functools.partial(ffn_kernel, order, n_b, count),
        name="ffn",
        compiler_params=limit(20 if n_e * rows <= ROWS else 40),
        cost_estimate=pl.CostEstimate(
            flops=6 * n_e * rows * w_gate.size, transcendentals=0, bytes_accessed=6 * w_gate.size
        ),
        out_shape=out_shape,
        in_specs=[VMEM] * (n_e + 3),
        out_specs=[VMEM] * n_b,
    )(*[xs[i] for i in order], w_gate, w_up, w_down)


def merge_kernel(order, *refs):
    parts, outs = restored(refs[: len(order)], order), refs[len(order) :]
    total = parts[0][...]
    for r in parts[1:]:
        total = total + r[...].astype(jnp.float32)
    count = total.shape[0] // len(outs)
    for m, out in enumerate(outs):
        out[...] = total[m * count : (m + 1) * count].astype(out.dtype)


def merge(parts, n_e):
    rows, width = parts[0].shape
    order = first_last(len(parts))
    return pl.pallas_call(
        functools.partial(merge_kernel, order),
        name="merge",
        compiler_params=limit(8),
        out_shape=[jax.ShapeDtypeStruct((rows // n_e, width), jnp.bfloat16)] * n_e,
        in_specs=[VMEM] * len(parts),
        out_specs=[VMEM] * n_e,
    )(*[parts[i] for i in order])


def mix_kernel(order, ids_ref, fixed_ref, *refs):
    blocks, out, n_e = restored(refs[:-1], order), refs[-1], len(order)
    me = lax.axis_index("expert")
    ids = ids_ref[...]
    fixed = fixed_ref[...].astype(jnp.float32)
    shares = fixed / jnp.sum(fixed, axis=1, keepdims=True)
    mixed = None
    for m, block in enumerate(blocks):
        share = jnp.sum(jnp.where(ids == source(me, m, n_e), shares, 0.0), axis=1, keepdims=True)
        part = share * block[...].astype(jnp.float32)
        mixed = part if m == 0 else mixed + part
    out[...] = mixed.astype(out.dtype)


def mix(route_ids, gate_fixed, blocks):
    order = half_first(len(blocks))
    return pl.pallas_call(
        functools.partial(mix_kernel, order),
        name="mix",
        compiler_params=limit(4),
        out_shape=jax.ShapeDtypeStruct(blocks[0].shape, jnp.bfloat16),
        in_specs=[VMEM] * (2 + len(blocks)),
        out_specs=VMEM,
    )(route_ids, gate_fixed, *[blocks[i] for i in order])


def on_device(tokens, route_ids, route_slots, gate_fixed, w_gate, w_up, w_down):
    count = tokens.shape[0]
    n_e, n_b = lax.axis_size("expert"), lax.axis_size("blk")
    mine, step = tokens, 1
    while step < n_b:
        more = fetch(mine[: (n_b - step) * count], "blk", step)
        mine = stack(on_chip(mine) if step == 1 else mine, more)
        step *= 2
    xs = [mine] + [fetch(mine, "expert", m) for m in range(1, n_e)]
    parts = ffn(xs, w_gate, w_up, w_down, n_b, count)
    parts = [parts[0]] + [deliver(parts[d], "blk", d) for d in range(1, n_b)]
    blocks = merge(parts, n_e)
    blocks = [blocks[0]] + [deliver(blocks[m], "expert", m) for m in range(1, n_e)]
    return mix(route_ids, gate_fixed, blocks)


def solution(mesh):
    return jax.shard_map(
        on_device,
        mesh=mesh,
        in_specs=(
            P(("group", "expert", "blk"), None),
            P(("group", "expert", "blk"), None),
            P(("group", "expert", "blk"), None),
            P(("group", "expert", "blk"), None),
            P("expert", None, "blk"),
            P("expert", None, "blk"),
            P("expert", "blk", None),
        ),
        out_specs=P(("group", "expert", "blk"), None),
        check_vma=False,
    )
```

```python
import functools

import jax
import jax.numpy as jnp
from jax import lax
from jax.experimental import pallas as pl
from jax.experimental.pallas import tpu as pltpu
from jax.sharding import PartitionSpec as P

ROWS = 128
HINT = 2 * 10**10
VMEM = pl.BlockSpec(memory_space=pltpu.VMEM)
ANY = pl.BlockSpec(memory_space=pl.ANY)


def limit(mib):
    return pltpu.CompilerParams(vmem_limit_bytes=mib << 20)


def peer(i, d, n):
    return i ^ d if n & (n - 1) == 0 else (i + d) % n


def source(i, d, n):
    return i ^ d if n & (n - 1) == 0 else (i - d) % n


def fetch(x, axis, d):
    n = lax.axis_size(axis)
    return lax.ppermute(x, axis, [(peer(i, d, n), i) for i in range(n)])


def deliver(x, axis, d):
    n = lax.axis_size(axis)
    return lax.ppermute(x, axis, [(i, peer(i, d, n)) for i in range(n)])


def last_first(n):
    return [0, n - 1, *range(1, n - 1)]


def half_first(n):
    return [0, n // 2, *(i for i in range(1, n) if i != n // 2)]


def restored(refs, order):
    got = [None] * len(order)
    for ref, i in zip(refs, order, strict=True):
        got[i] = ref
    return got


def rows_kernel(src, dst, sem):
    copy = pltpu.make_async_copy(src, dst, sem)
    copy.start()
    copy.wait()


def on_chip(x):
    return pl.pallas_call(
        rows_kernel,
        name="rows",
        compiler_params=limit(1),
        cost_estimate=pl.CostEstimate(flops=0, transcendentals=0, bytes_accessed=4 * x.size),
        out_shape=pltpu.VMEM(x.shape, x.dtype),
        in_specs=[ANY],
        out_specs=VMEM,
        scratch_shapes=[pltpu.SemaphoreType.DMA],
    )(pltpu.with_memory_space_constraint(x, pltpu.HBM))


def stack_kernel(upper, lower, out):
    rows = [r[...].astype(jnp.float32) for r in (upper, lower)]
    out[...] = jnp.concatenate(rows, axis=0).astype(out.dtype)


def stack(upper, lower):
    rows = upper.shape[0] + lower.shape[0]
    return pl.pallas_call(
        stack_kernel,
        name="stack",
        compiler_params=limit(1 if rows * upper.shape[1] < 2**16 else 8),
        cost_estimate=pl.CostEstimate(flops=HINT, transcendentals=0, bytes_accessed=0),
        out_shape=jax.ShapeDtypeStruct((rows, upper.shape[1]), upper.dtype),
        in_specs=[VMEM] * 2,
        out_specs=VMEM,
    )(upper, lower)


def ffn_kernel(order, n_e, n_b, count, *refs):
    xs, refs = restored(refs[: len(order)], order), refs[len(order) :]
    (gate_w, up_w, down_w), outs = refs[:3], refs[3:]
    x = jnp.concatenate([r[...] for r in xs], axis=0)
    spare = -x.shape[0] % ROWS
    if spare:
        x = jnp.concatenate([x, jnp.zeros((spare, x.shape[1]), x.dtype)], axis=0)
    v = jnp.dot(x, gate_w[0], preferred_element_type=jnp.float32)
    u = jnp.dot(x, up_w[0], preferred_element_type=jnp.float32)
    hidden = (v / (1.0 + jnp.exp(-v)) * u).astype(jnp.bfloat16)
    total = jnp.dot(hidden, down_w[0], preferred_element_type=jnp.float32)
    for d, out in enumerate(outs):
        part = [total[(m * n_b + d) * count : (m * n_b + d + 1) * count] for m in range(n_e)]
        out[...] = jnp.concatenate(part, axis=0).astype(out.dtype)


def ffn(xs, w_gate, w_up, w_down, n_e, n_b, count):
    rows, width = n_b * count, xs[0].shape[1]
    pieces = len(xs) // n_e
    order = [m * pieces + p for p in range(pieces) for m in range(n_e)]
    out_shape = [
        jax.ShapeDtypeStruct((n_e * count, width), jnp.float32 if d == 0 else jnp.bfloat16) for d in range(n_b)
    ]
    return pl.pallas_call(
        functools.partial(ffn_kernel, order, n_e, n_b, count),
        name="ffn",
        compiler_params=limit(20 if n_e * rows <= ROWS else 40),
        cost_estimate=pl.CostEstimate(
            flops=6 * n_e * rows * w_gate.size, transcendentals=0, bytes_accessed=6 * w_gate.size
        ),
        out_shape=out_shape,
        in_specs=[VMEM] * (len(xs) + 3),
        out_specs=[VMEM] * n_b,
    )(*[xs[i] for i in order], w_gate, w_up, w_down)


def merge_kernel(order, *refs):
    parts, outs = restored(refs[: len(order)], order), refs[len(order) :]
    total = parts[0][...]
    for r in parts[1:]:
        total = total + r[...].astype(jnp.float32)
    count = total.shape[0] // len(outs)
    for m, out in enumerate(outs):
        out[...] = total[m * count : (m + 1) * count].astype(out.dtype)


def merge(parts, n_e):
    rows, width = parts[0].shape
    order = last_first(len(parts))
    return pl.pallas_call(
        functools.partial(merge_kernel, order),
        name="merge",
        compiler_params=limit(8),
        out_shape=[jax.ShapeDtypeStruct((rows // n_e, width), jnp.bfloat16)] * n_e,
        in_specs=[VMEM] * len(parts),
        out_specs=[VMEM] * n_e,
    )(*[parts[i] for i in order])


def mix_kernel(order, ids_ref, fixed_ref, *refs):
    blocks, out, n_e = restored(refs[:-1], order), refs[-1], len(order)
    me = lax.axis_index("expert")
    ids = ids_ref[...]
    fixed = fixed_ref[...].astype(jnp.float32)
    shares = fixed / jnp.sum(fixed, axis=1, keepdims=True)
    mixed = None
    for m, block in enumerate(blocks):
        share = jnp.sum(jnp.where(ids == source(me, m, n_e), shares, 0.0), axis=1, keepdims=True)
        part = share * block[...].astype(jnp.float32)
        mixed = part if m == 0 else mixed + part
    out[...] = mixed.astype(out.dtype)


def mix(route_ids, gate_fixed, blocks):
    order = half_first(len(blocks))
    return pl.pallas_call(
        functools.partial(mix_kernel, order),
        name="mix",
        compiler_params=limit(4),
        out_shape=jax.ShapeDtypeStruct(blocks[0].shape, jnp.bfloat16),
        in_specs=[VMEM] * (2 + len(blocks)),
        out_specs=VMEM,
    )(route_ids, gate_fixed, *[blocks[i] for i in order])


def on_device(tokens, route_ids, route_slots, gate_fixed, w_gate, w_up, w_down):
    count = tokens.shape[0]
    n_e, n_b = lax.axis_size("expert"), lax.axis_size("blk")
    mine, step = tokens, 1
    while 2 * step < n_b:
        more = fetch(mine[: (n_b - step) * count], "blk", step)
        mine = stack(on_chip(mine) if step == 1 else mine, more)
        step *= 2
    pieces = [mine] if n_b == step else [mine, fetch(mine[: (n_b - step) * count], "blk", step)]
    xs = [fetch(piece, "expert", m) if m else piece for m in range(n_e) for piece in pieces]
    parts = ffn(xs, w_gate, w_up, w_down, n_e, n_b, count)
    parts = [parts[0]] + [deliver(parts[d], "blk", d) for d in range(1, n_b)]
    blocks = merge(parts, n_e)
    blocks = [blocks[0]] + [deliver(blocks[m], "expert", m) for m in range(1, n_e)]
    return mix(route_ids, gate_fixed, blocks)


def solution(mesh):
    return jax.shard_map(
        on_device,
        mesh=mesh,
        in_specs=(
            P(("group", "expert", "blk"), None),
            P(("group", "expert", "blk"), None),
            P(("group", "expert", "blk"), None),
            P(("group", "expert", "blk"), None),
            P("expert", None, "blk"),
            P("expert", None, "blk"),
            P("expert", "blk", None),
        ),
        out_specs=P(("group", "expert", "blk"), None),
        check_vma=False,
    )
```

```python
import functools

import jax
import jax.numpy as jnp
from jax import lax
from jax.experimental import pallas as pl
from jax.experimental.pallas import tpu as pltpu
from jax.sharding import PartitionSpec as P

ROWS = 128
HINT = 2 * 10**10
VMEM = pl.BlockSpec(memory_space=pltpu.VMEM)
ANY = pl.BlockSpec(memory_space=pl.ANY)


def limit(mib):
    return pltpu.CompilerParams(vmem_limit_bytes=mib << 20)


def peer(i, d, n):
    return i ^ d if n & (n - 1) == 0 else (i + d) % n


def source(i, d, n):
    return i ^ d if n & (n - 1) == 0 else (i - d) % n


def fetch(x, axis, d):
    n = lax.axis_size(axis)
    return lax.ppermute(x, axis, [(peer(i, d, n), i) for i in range(n)])


def deliver(x, axis, d):
    n = lax.axis_size(axis)
    return lax.ppermute(x, axis, [(i, peer(i, d, n)) for i in range(n)])


def last_first(n):
    return [0, n - 1, *range(1, n - 1)]


def falling(n):
    return [0, *range(n - 1, 0, -1)]


def restored(refs, order):
    got = [None] * len(order)
    for ref, i in zip(refs, order, strict=True):
        got[i] = ref
    return got


def rows_kernel(src, dst, sem):
    copy = pltpu.make_async_copy(src, dst, sem)
    copy.start()
    copy.wait()


def on_chip(x):
    return pl.pallas_call(
        rows_kernel,
        name="rows",
        compiler_params=limit(1),
        cost_estimate=pl.CostEstimate(flops=0, transcendentals=0, bytes_accessed=4 * x.size),
        out_shape=pltpu.VMEM(x.shape, x.dtype),
        in_specs=[ANY],
        out_specs=VMEM,
        scratch_shapes=[pltpu.SemaphoreType.DMA],
    )(pltpu.with_memory_space_constraint(x, pltpu.HBM))


def stack_kernel(upper, lower, out):
    rows = [r[...].astype(jnp.float32) for r in (upper, lower)]
    out[...] = jnp.concatenate(rows, axis=0).astype(out.dtype)


def stack(upper, lower):
    rows = upper.shape[0] + lower.shape[0]
    return pl.pallas_call(
        stack_kernel,
        name="stack",
        compiler_params=limit(1 if rows * upper.shape[1] < 2**16 else 8),
        cost_estimate=pl.CostEstimate(flops=HINT, transcendentals=0, bytes_accessed=0),
        out_shape=jax.ShapeDtypeStruct((rows, upper.shape[1]), upper.dtype),
        in_specs=[VMEM] * 2,
        out_specs=VMEM,
    )(upper, lower)


def ffn_kernel(order, n_e, n_b, count, *refs):
    xs, refs = restored(refs[: len(order)], order), refs[len(order) :]
    (gate_w, up_w, down_w), outs = refs[:3], refs[3:]
    x = jnp.concatenate([r[...] for r in xs], axis=0)
    spare = -x.shape[0] % ROWS
    if spare:
        x = jnp.concatenate([x, jnp.zeros((spare, x.shape[1]), x.dtype)], axis=0)
    v = jnp.dot(x, gate_w[0], preferred_element_type=jnp.float32)
    u = jnp.dot(x, up_w[0], preferred_element_type=jnp.float32)
    hidden = (v / (1.0 + jnp.exp(-v)) * u).astype(jnp.bfloat16)
    total = jnp.dot(hidden, down_w[0], preferred_element_type=jnp.float32)
    for d, out in enumerate(outs):
        part = [total[(m * n_b + d) * count : (m * n_b + d + 1) * count] for m in range(n_e)]
        out[...] = jnp.concatenate(part, axis=0).astype(out.dtype)


def ffn(xs, w_gate, w_up, w_down, n_e, n_b, count):
    rows, width = n_b * count, xs[0].shape[1]
    pieces = len(xs) // n_e
    order = [m * pieces + p for p in range(pieces) for m in range(n_e)]
    out_shape = [
        jax.ShapeDtypeStruct((n_e * count, width), jnp.float32 if d == 0 else jnp.bfloat16) for d in range(n_b)
    ]
    return pl.pallas_call(
        functools.partial(ffn_kernel, order, n_e, n_b, count),
        name="ffn",
        compiler_params=limit(20 if n_e * rows <= ROWS else 40),
        cost_estimate=pl.CostEstimate(
            flops=6 * n_e * rows * w_gate.size, transcendentals=0, bytes_accessed=6 * w_gate.size
        ),
        out_shape=out_shape,
        in_specs=[VMEM] * (len(xs) + 3),
        out_specs=[VMEM] * n_b,
    )(*[xs[i] for i in order], w_gate, w_up, w_down)


def merge_kernel(order, *refs):
    parts, outs = restored(refs[: len(order)], order), refs[len(order) :]
    total = parts[0][...]
    for r in parts[1:]:
        total = total + r[...].astype(jnp.float32)
    count = total.shape[0] // len(outs)
    for m, out in enumerate(outs):
        out[...] = total[m * count : (m + 1) * count].astype(out.dtype)


def merge(parts, n_e):
    rows, width = parts[0].shape
    order = last_first(len(parts))
    return pl.pallas_call(
        functools.partial(merge_kernel, order),
        name="merge",
        compiler_params=limit(8),
        out_shape=[jax.ShapeDtypeStruct((rows // n_e, width), jnp.bfloat16)] * n_e,
        in_specs=[VMEM] * len(parts),
        out_specs=[VMEM] * n_e,
    )(*[parts[i] for i in order])


def mix_kernel(order, ids_ref, fixed_ref, *refs):
    blocks, out, n_e = restored(refs[:-1], order), refs[-1], len(order)
    me = lax.axis_index("expert")
    ids = ids_ref[...]
    fixed = fixed_ref[...].astype(jnp.float32)
    shares = fixed / jnp.sum(fixed, axis=1, keepdims=True)
    mixed = None
    for m, block in enumerate(blocks):
        share = jnp.sum(jnp.where(ids == source(me, m, n_e), shares, 0.0), axis=1, keepdims=True)
        part = share * block[...].astype(jnp.float32)
        mixed = part if m == 0 else mixed + part
    out[...] = mixed.astype(out.dtype)


def mix(route_ids, gate_fixed, blocks):
    order = falling(len(blocks))
    return pl.pallas_call(
        functools.partial(mix_kernel, order),
        name="mix",
        compiler_params=limit(4),
        out_shape=jax.ShapeDtypeStruct(blocks[0].shape, jnp.bfloat16),
        in_specs=[VMEM] * (2 + len(blocks)),
        out_specs=VMEM,
    )(route_ids, gate_fixed, *[blocks[i] for i in order])


def on_device(tokens, route_ids, route_slots, gate_fixed, w_gate, w_up, w_down):
    count = tokens.shape[0]
    n_e, n_b = lax.axis_size("expert"), lax.axis_size("blk")
    mine, step = tokens, 1
    while 2 * step < n_b:
        more = fetch(mine[: (n_b - step) * count], "blk", step)
        mine = stack(on_chip(mine) if step == 1 else mine, more)
        step *= 2
    pieces = [mine] if n_b == step else [mine, fetch(mine[: (n_b - step) * count], "blk", step)]
    xs = [fetch(piece, "expert", m) if m else piece for m in range(n_e) for piece in pieces]
    parts = ffn(xs, w_gate, w_up, w_down, n_e, n_b, count)
    parts = [parts[0]] + [deliver(parts[d], "blk", d) for d in range(1, n_b)]
    blocks = merge(parts, n_e)
    blocks = [blocks[0]] + [deliver(blocks[m], "expert", m) for m in range(1, n_e)]
    return mix(route_ids, gate_fixed, blocks)


def solution(mesh):
    return jax.shard_map(
        on_device,
        mesh=mesh,
        in_specs=(
            P(("group", "expert", "blk"), None),
            P(("group", "expert", "blk"), None),
            P(("group", "expert", "blk"), None),
            P(("group", "expert", "blk"), None),
            P("expert", None, "blk"),
            P("expert", None, "blk"),
            P("expert", "blk", None),
        ),
        out_specs=P(("group", "expert", "blk"), None),
        check_vma=False,
    )
```

```python
import functools

import jax
import jax.numpy as jnp
from jax import lax
from jax.experimental import pallas as pl
from jax.experimental.pallas import tpu as pltpu
from jax.sharding import PartitionSpec as P

ROWS = 128
HINT = 2 * 10**10
VMEM = pl.BlockSpec(memory_space=pltpu.VMEM)
ANY = pl.BlockSpec(memory_space=pl.ANY)


def limit(mib):
    return pltpu.CompilerParams(vmem_limit_bytes=mib << 20)


def peer(i, d, n):
    return i ^ d if n & (n - 1) == 0 else (i + d) % n


def source(i, d, n):
    return i ^ d if n & (n - 1) == 0 else (i - d) % n


def fetch(x, axis, d):
    n = lax.axis_size(axis)
    return lax.ppermute(x, axis, [(peer(i, d, n), i) for i in range(n)])


def deliver(x, axis, d):
    n = lax.axis_size(axis)
    return lax.ppermute(x, axis, [(i, peer(i, d, n)) for i in range(n)])


def last_first(n):
    return [0, n - 1, *range(1, n - 1)]


def half_first(n):
    return [0, n // 2, *(i for i in range(1, n) if i != n // 2)]


def restored(refs, order):
    got = [None] * len(order)
    for ref, i in zip(refs, order, strict=True):
        got[i] = ref
    return got


def rows_kernel(src, dst, sem):
    copy = pltpu.make_async_copy(src, dst, sem)
    copy.start()
    copy.wait()


def on_chip(x):
    return pl.pallas_call(
        rows_kernel,
        name="rows",
        compiler_params=limit(1),
        cost_estimate=pl.CostEstimate(flops=0, transcendentals=0, bytes_accessed=4 * x.size),
        out_shape=pltpu.VMEM(x.shape, x.dtype),
        in_specs=[ANY],
        out_specs=VMEM,
        scratch_shapes=[pltpu.SemaphoreType.DMA],
    )(pltpu.with_memory_space_constraint(x, pltpu.HBM))


def stack_kernel(upper, lower, out):
    rows = [r[...].astype(jnp.float32) for r in (upper, lower)]
    out[...] = jnp.concatenate(rows, axis=0).astype(out.dtype)


def stack(upper, lower):
    rows = upper.shape[0] + lower.shape[0]
    return pl.pallas_call(
        stack_kernel,
        name="stack",
        compiler_params=limit(1 if rows * upper.shape[1] < 2**16 else 8),
        cost_estimate=pl.CostEstimate(flops=HINT, transcendentals=0, bytes_accessed=0),
        out_shape=jax.ShapeDtypeStruct((rows, upper.shape[1]), upper.dtype),
        in_specs=[VMEM] * 2,
        out_specs=VMEM,
    )(upper, lower)


def ffn_kernel(order, n_e, n_b, count, *refs):
    xs, refs = restored(refs[: len(order)], order), refs[len(order) :]
    (gate_w, up_w, down_w), outs = refs[:3], refs[3:]
    x = jnp.concatenate([r[...] for r in xs], axis=0)
    spare = -x.shape[0] % ROWS
    if spare:
        x = jnp.concatenate([x, jnp.zeros((spare, x.shape[1]), x.dtype)], axis=0)
    v = jnp.dot(x, gate_w[0], preferred_element_type=jnp.float32)
    u = jnp.dot(x, up_w[0], preferred_element_type=jnp.float32)
    hidden = (v / (1.0 + jnp.exp(-v)) * u).astype(jnp.bfloat16)
    total = jnp.dot(hidden, down_w[0], preferred_element_type=jnp.float32)
    for d, out in enumerate(outs):
        part = [total[(m * n_b + d) * count : (m * n_b + d + 1) * count] for m in range(n_e)]
        out[...] = jnp.concatenate(part, axis=0).astype(out.dtype)


def ffn(xs, w_gate, w_up, w_down, n_e, n_b, count):
    rows, width = n_b * count, xs[0].shape[1]
    pieces = len(xs) // n_e
    order = [m * pieces + p for p in range(pieces) for m in range(n_e)]
    out_shape = [
        jax.ShapeDtypeStruct((n_e * count, width), jnp.float32 if d == 0 else jnp.bfloat16) for d in range(n_b)
    ]
    return pl.pallas_call(
        functools.partial(ffn_kernel, order, n_e, n_b, count),
        name="ffn",
        compiler_params=limit(20 if n_e * rows <= ROWS else 40),
        cost_estimate=pl.CostEstimate(
            flops=6 * n_e * rows * w_gate.size, transcendentals=0, bytes_accessed=6 * w_gate.size
        ),
        out_shape=out_shape,
        in_specs=[VMEM] * (len(xs) + 3),
        out_specs=[VMEM] * n_b,
    )(*[xs[i] for i in order], w_gate, w_up, w_down)


def merge_kernel(order, *refs):
    parts, outs = restored(refs[: len(order)], order), refs[len(order) :]
    total = parts[0][...]
    for r in parts[1:]:
        total = total + r[...].astype(jnp.float32)
    count = total.shape[0] // len(outs)
    for m, out in enumerate(outs):
        out[...] = total[m * count : (m + 1) * count].astype(out.dtype)


def merge(parts, n_e):
    rows, width = parts[0].shape
    order = last_first(len(parts))
    return pl.pallas_call(
        functools.partial(merge_kernel, order),
        name="merge",
        compiler_params=limit(8),
        out_shape=[jax.ShapeDtypeStruct((rows // n_e, width), jnp.bfloat16)] * n_e,
        in_specs=[VMEM] * len(parts),
        out_specs=[VMEM] * n_e,
    )(*[parts[i] for i in order])


def shares_kernel(n_e, ids_ref, fixed_ref, out):
    me = lax.axis_index("expert")
    ids = ids_ref[...]
    fixed = fixed_ref[...].astype(jnp.float32)
    shares = fixed / jnp.sum(fixed, axis=1, keepdims=True)
    for m in range(n_e):
        share = jnp.sum(jnp.where(ids == source(me, m, n_e), shares, 0.0), axis=1, keepdims=True)
        out[m] = jnp.broadcast_to(share, out.shape[1:])


def shares_of(route_ids, gate_fixed, n_e):
    return pl.pallas_call(
        functools.partial(shares_kernel, n_e),
        name="shares",
        compiler_params=limit(1),
        out_shape=jax.ShapeDtypeStruct((n_e, route_ids.shape[0], 128), jnp.float32),
        in_specs=[VMEM] * 2,
        out_specs=VMEM,
    )(route_ids, gate_fixed)


def mix_kernel(order, shares, *refs):
    blocks, out = restored(refs[:-1], order), refs[-1]
    mixed = None
    for m, block in enumerate(blocks):
        part = shares[m, :, :1] * block[...].astype(jnp.float32)
        mixed = part if m == 0 else mixed + part
    out[...] = mixed.astype(out.dtype)


def mix(shares, blocks):
    order = half_first(len(blocks))
    return pl.pallas_call(
        functools.partial(mix_kernel, order),
        name="mix",
        compiler_params=limit(4),
        out_shape=jax.ShapeDtypeStruct(blocks[0].shape, jnp.bfloat16),
        in_specs=[VMEM] * (1 + len(blocks)),
        out_specs=VMEM,
    )(shares, *[blocks[i] for i in order])


def on_device(tokens, route_ids, route_slots, gate_fixed, w_gate, w_up, w_down):
    count = tokens.shape[0]
    n_e, n_b = lax.axis_size("expert"), lax.axis_size("blk")
    mine, step = tokens, 1
    while 2 * step < n_b:
        more = fetch(mine[: (n_b - step) * count], "blk", step)
        mine = stack(on_chip(mine) if step == 1 else mine, more)
        step *= 2
    pieces = [mine] if n_b == step else [mine, fetch(mine[: (n_b - step) * count], "blk", step)]
    xs = [fetch(piece, "expert", m) if m else piece for m in range(n_e) for piece in pieces]
    parts = ffn(xs, w_gate, w_up, w_down, n_e, n_b, count)
    parts = [parts[0]] + [deliver(parts[d], "blk", d) for d in range(1, n_b)]
    blocks = merge(parts, n_e)
    blocks = [blocks[0]] + [deliver(blocks[m], "expert", m) for m in range(1, n_e)]
    return mix(shares_of(route_ids, gate_fixed, n_e), blocks)


def solution(mesh):
    return jax.shard_map(
        on_device,
        mesh=mesh,
        in_specs=(
            P(("group", "expert", "blk"), None),
            P(("group", "expert", "blk"), None),
            P(("group", "expert", "blk"), None),
            P(("group", "expert", "blk"), None),
            P("expert", None, "blk"),
            P("expert", None, "blk"),
            P("expert", "blk", None),
        ),
        out_specs=P(("group", "expert", "blk"), None),
        check_vma=False,
    )
```
